32 devices in a mesh: groups: 2 (over x), space: 16 (over z, y, core).
Axes of the slice: x: 2, y: 2, z: 4, core: 2. Of those that a mesh axis runs over, the one named last changes fastest.
Arguments:
- eigvecs: bfloat16 [32, 64, 2, 3, 128], P('groups', 'space'), parts along dimension 0, may hold values from -1.3515625 to 1.3515625
- phase_index: int32 [128], P('groups'), parts along dimension 0, may hold values from 0 to 47
- perambulator: bfloat16 [512, 2, 128, 128], P(('groups', 'space')), parts along dimension 0, may hold values from -0.046875 to 0.046875
- tile_sink: int32 [512, 1], P(('groups', 'space')), parts along dimension 0, may hold values from 0 to 15; in each aligned block of 16 rows (0 to 15, 16 to 31, ...) at most 2 rows name the same one
- tile_sep: int32 [512], P(('groups', 'space')), parts along dimension 0, may hold values from 0 to 7
- tile_diagram: int32 [512], P(('groups', 'space')), parts along dimension 0, may hold values from 0 to 1
Outputs:
- elementals: bfloat16 [32, 2, 128, 128], P(('groups', 'space')), parts along dimension 0
- correlator: float32 [512, 2], P(('groups', 'space')), parts along dimension 0
The draws below stay inside these ranges and needn't reach their ends.
There are 2 independent parts, one for each index of `groups`. The reference program is written for one: setup_inputs(seed, part) draws one part's arguments, and reference() takes and returns one part's arrays. A program takes and returns all parts, laid end to end along the dimension named above; each array names one. Nothing has to cross between parts.
Inputs may be any that keep to these rules, and one draw needn't show every extreme that they name: `tile_sink`: in the tiles of one device no sink time is named by more than 2 tiles.
All inputs are finite; a program needn't handle non-finite values.
Results may differ from the reference program's by a relative error of at most 0.0048.
Values may be sent and summed in bfloat16 or wider, within the bound.
A program may use at most 128 MiB of HBM per device.

```python
import math
import jax
import jax.numpy as jnp
import numpy as np
from jax import lax

NVEC = 128
COLORS = 3
PERIOD = 48
SEP = 8
CAP = 2
TIME = 16
SITES = 64
TILE_DEV = 16
TILES = 256


def with_ends(entries, stream_key, least, largest):
    longest = entries.shape.index(max(entries.shape))
    spots = []
    for shift in (0, 1):
        where = [jax.random.randint(jax.random.fold_in(stream_key, axis), (), 0, length) for axis, length in enumerate(entries.shape)]
        where[longest] = (where[longest] + shift) % entries.shape[longest]
        spots.append(tuple(where))
    return entries.at[spots[0]].set(least).at[spots[1]].set(largest)


def block_levels(rng, extent, split, low, top_value):
    gain = 1.0
    for dim, blocks in split:
        heights = jax.random.uniform(jax.random.fold_in(jax.random.fold_in(rng, 6), dim), (blocks,), jnp.float32, low / len(split), top_value / len(split))
        gain = gain * jnp.repeat(jnp.exp(heights), extent[dim] // blocks).reshape((-1,) + (1,) * (len(extent) - 1 - dim))
    return gain


def shared_out(rng, own, number, rows, count, top, limit, lean):
    sequence = jax.random.permutation(rng, count)
    crowded, ordinary = load_shares(count, rows * top, limit, lean, True), load_shares(count, rows * top, limit, lean, False)
    places = jnp.arange(count)

    def named(lengths, rotation):
        used = int((lengths > 0).sum())
        fixed = max(1, used // 4)
        moved = fixed + (places - fixed + rotation * (used - fixed)) % max(1, count - fixed)
        return jnp.zeros((count,), jnp.int32).at[sequence[jnp.where(places < fixed, places, moved)]].set(jnp.asarray(lengths, jnp.int32))

    lengths = jnp.where(number % 4 == 0, named(crowded, number // 4), named(ordinary, number - number // 4 - 1))
    mixed = jax.random.permutation(jax.random.fold_in(own, 3), count)
    donor, taker = mixed[0:count // 2 * 2:2], mixed[1:count // 2 * 2:2]
    slack = jnp.minimum(lengths[donor] - 1, limit - lengths[taker]) // 2
    slack = jnp.where((donor == sequence[0]) | (taker == sequence[0]) | (lengths[taker] == 0), 0, jnp.maximum(slack, 0))
    moved = jax.random.randint(jax.random.fold_in(own, 4), (count // 2,), 0, 1 << 20) % (slack + 1)
    lengths = lengths.at[donor].add(-moved).at[taker].add(moved)
    labels = jnp.searchsorted(jnp.cumsum(lengths), jnp.arange(rows * top), side="right").astype(jnp.int32)
    grid = labels.reshape(top, rows).T
    grid = grid[jax.random.permutation(jax.random.fold_in(own, 1), rows)]
    rotation = jax.random.randint(jax.random.fold_in(own, 2), (rows, 1), 0, top)
    return jnp.take_along_axis(grid, (jnp.arange(top)[None, :] + rotation) % top, axis=1)


def load_shares(count, total, bound, lean, full):
    loads = [(1 << 20) // math.isqrt(standing ** lean) + 1 for standing in range(1, count + 1)]
    largest = bound if full else min(bound, max(-(-total // count), total * loads[0] // sum(loads)))
    least = 1 if total - largest >= count - 1 else 0
    holding, rest = [largest] + [least] * (count - 1), total - largest - least * (count - 1)
    while rest > 0:
        free = [i for i in range(1, count) if holding[i] < largest] or [i for i in range(1, count) if holding[i] < bound]
        mass, remaining = sum([loads[i] for i in free]), rest
        for i in free:
            addition = min(bound - holding[i], max(1, remaining * loads[i] // mass), rest)
            holding[i] = holding[i] + addition
            rest = rest - addition
    return np.array(holding)


def normal_values(own_key, shape, deviation, most, cuts=(), held_as=jnp.bfloat16):
    array = deviation * jax.random.normal(own_key, shape, jnp.float32)
    if cuts:
        array = array * block_levels(own_key, shape, cuts, -0.22, 0.18)
    return jnp.clip(array, -most, most).astype(held_as)


def setup_inputs(seed: int = 0, part: int = 0) -> dict:
    streams_of = jax.random.split(jax.random.key(seed), 7)
    own_keys = jax.random.split(jax.random.fold_in(streams_of[6], part), 7)
    eigvecs = normal_values(own_keys[0], (TIME, SITES, 2, COLORS, NVEC), (1.0 / (6 * SITES) ** 0.25), 1.3515625, ((1, 16),))
    phase_index = with_ends(jax.random.randint(own_keys[1], (SITES,), 0, PERIOD), jax.random.fold_in(own_keys[1], 1), 0, PERIOD - 1).astype(jnp.int32)
    perambulator = normal_values(own_keys[2], (TILES, 2, NVEC, NVEC), 0.0078125, 0.046875, ((0, 16),))
    tile_sink_keys = jax.random.split(jax.random.fold_in(own_keys[3], 1), TILES // TILE_DEV)
    tile_sink_turns = jax.random.permutation(jax.random.fold_in(own_keys[3], 3), TILES // TILE_DEV)
    tile_sink = jax.vmap(lambda own, number: shared_out(jax.random.fold_in(own_keys[3], 2), own, number, TILE_DEV, TIME, 1, CAP, 2))(tile_sink_keys, tile_sink_turns).reshape((TILES, 1))
    tile_sep = with_ends(jax.random.randint(own_keys[4], (TILES,), 0, SEP), jax.random.fold_in(own_keys[4], 1), 0, SEP - 1).astype(jnp.int32)
    tile_diagram = with_ends(jax.random.randint(own_keys[5], (TILES,), 0, 2), jax.random.fold_in(own_keys[5], 1), 0, 1).astype(jnp.int32)
    return dict(eigvecs=eigvecs, phase_index=phase_index, perambulator=perambulator, tile_sink=tile_sink, tile_sep=tile_sep, tile_diagram=tile_diagram)


def make_right(vecs, cosine, sine):
    real_part = vecs[..., 0, :, :].astype(jnp.float32)
    imag_part = vecs[..., 1, :, :].astype(jnp.float32)
    cos_col = cosine[:, None, None]
    sin_col = sine[:, None, None]
    first = (cos_col * real_part - sin_col * imag_part).astype(jnp.bfloat16)
    second = (sin_col * real_part + cos_col * imag_part).astype(jnp.bfloat16)
    top = jnp.stack([first, second], -2)
    bottom = jnp.stack([second, -first], -2)
    return jnp.stack([top, bottom], -4)


def contract_tiles(sink_mat, source_mat, tiles, diagram):
    def mult(left, right):
        return jnp.einsum("bij,bjk->bik", left.astype(jnp.float32), right.astype(jnp.float32))

    tile_re = tiles[:, 0]
    tile_im = tiles[:, 1]
    trans_re = jnp.swapaxes(tile_re, 1, 2)
    trans_im = -jnp.swapaxes(tile_im, 1, 2)
    flag = (diagram == 1)[:, None, None]
    left_re = jnp.where(flag, trans_re, tile_re)
    left_im = jnp.where(flag, trans_im, tile_im)
    right_re = jnp.where(flag, tile_re, trans_re)
    right_im = jnp.where(flag, tile_im, trans_im)
    sink_re = sink_mat[:, 0]
    sink_im = sink_mat[:, 1]
    src_re = jnp.swapaxes(source_mat[:, 0], 1, 2)
    src_im = -jnp.swapaxes(source_mat[:, 1], 1, 2)
    first_re = mult(sink_re, left_re) - mult(sink_im, left_im)
    first_im = mult(sink_re, left_im) + mult(sink_im, left_re)
    second_re = mult(src_re, right_re) - mult(src_im, right_im)
    second_im = mult(src_re, right_im) + mult(src_im, right_re)
    second_re = jnp.swapaxes(second_re, 1, 2)
    second_im = jnp.swapaxes(second_im, 1, 2)
    trace_re = jnp.sum(first_re * second_re - first_im * second_im, axis=(1, 2))
    trace_im = jnp.sum(first_re * second_im + first_im * second_re, axis=(1, 2))
    return jnp.stack([trace_re, trace_im], -1)


def reference(eigvecs, phase_index, perambulator, tile_sink, tile_sep, tile_diagram):
    angle = (2.0 * math.pi / PERIOD) * phase_index.astype(jnp.float32)
    cosine = jnp.cos(angle)
    sine = jnp.sin(angle)

    def one_slice(vecs):
        right = make_right(vecs, cosine, sine)
        value = jnp.einsum("spck,spcol->okl", vecs.astype(jnp.float32), right.astype(jnp.float32))
        return value.astype(jnp.bfloat16)

    elementals = lax.map(one_slice, eigvecs)
    total = perambulator.shape[0]
    block = math.gcd(32, total)
    sinks = tile_sink[:, 0].astype(jnp.int32)
    sources = jnp.mod(sinks - tile_sep, TIME).astype(jnp.int32)

    def one_block(items):
        tiles, sink_ids, source_ids, diagram = items
        return contract_tiles(elementals[sink_ids], elementals[source_ids], tiles, diagram)

    shaped = (perambulator.reshape((total // block, block) + perambulator.shape[1:]),
              sinks.reshape(total // block, block), sources.reshape(total // block, block),
              tile_diagram.reshape(total // block, block))
    correlator = lax.map(one_block, shaped).reshape(total, 2)
    return elementals, correlator
```

```python
import functools
import math

import jax
import jax.numpy as jnp
from jax import lax
from jax.experimental import pallas as pl
from jax.experimental.pallas import tpu as pltpu
from jax.sharding import PartitionSpec as P

PERIOD = 48


def make_right(vecs, cosine, sine):
    real_part = vecs[..., 0, :, :].astype(jnp.float32)
    imag_part = vecs[..., 1, :, :].astype(jnp.float32)
    cos_col = cosine[:, None, None]
    sin_col = sine[:, None, None]
    first = (cos_col * real_part - sin_col * imag_part).astype(jnp.bfloat16)
    second = (sin_col * real_part + cos_col * imag_part).astype(jnp.bfloat16)
    top = jnp.stack([first, second], -2)
    bottom = jnp.stack([second, -first], -2)
    return jnp.stack([top, bottom], -4)


def phases(indices):
    angle = 2.0 * math.pi / PERIOD * indices.astype(jnp.float32)
    return (jnp.cos(angle), jnp.sin(angle))


def contract_tiles(sink_mat, source_mat, tiles, diagram):

    def mult(left, right):
        return jnp.einsum("bij,bjk->bik", left, right, preferred_element_type=jnp.float32)

    tile_re = tiles[:, 0]
    tile_im = tiles[:, 1]
    trans_re = jnp.swapaxes(tile_re, 1, 2)
    trans_im = -jnp.swapaxes(tile_im, 1, 2)
    flag = (diagram == 1)[:, None, None]
    left_re = jnp.where(flag, trans_re, tile_re)
    left_im = jnp.where(flag, trans_im, tile_im)
    right_re = jnp.where(flag, tile_re, trans_re)
    right_im = jnp.where(flag, tile_im, trans_im)
    sink_re = sink_mat[:, 0]
    sink_im = sink_mat[:, 1]
    src_re = jnp.swapaxes(source_mat[:, 0], 1, 2)
    src_im = -jnp.swapaxes(source_mat[:, 1], 1, 2)
    first_re = mult(sink_re, left_re) - mult(sink_im, left_im)
    first_im = mult(sink_re, left_im) + mult(sink_im, left_re)
    second_re = jnp.swapaxes(mult(src_re, right_re) - mult(src_im, right_im), 1, 2)
    second_im = jnp.swapaxes(mult(src_re, right_im) + mult(src_im, right_re), 1, 2)
    trace_re = jnp.sum(first_re * second_re - first_im * second_im, axis=(1, 2))
    trace_im = jnp.sum(first_re * second_im + first_im * second_re, axis=(1, 2))
    return jnp.stack([trace_re, trace_im], -1)


def run_blocks(step_fn, items, total):
    block = math.gcd(32, total)
    shaped = tuple((item.reshape((total // block, block) + item.shape[1:]) for item in items))
    result = lax.map(step_fn, shaped)
    return result.reshape((total,) + result.shape[2:])


def local_large(eigvecs, phase_index, perambulator, tile_sink, tile_sep, tile_diagram):
    tile_count = perambulator.shape[0]
    sinks = tile_sink[:, 0]
    cosine, sine = phases(phase_index)
    slices = lax.all_to_all(eigvecs, "space", split_axis=0, concat_axis=1, tiled=True)
    vecs = slices[0]
    right = make_right(vecs, cosine, sine)
    value = jnp.einsum("spck,spcol->okl", vecs, right, preferred_element_type=jnp.float32)
    elemental = value.astype(jnp.bfloat16)[None]
    gathered = lax.all_gather(elemental, "space", axis=0, tiled=True)
    time_count = gathered.shape[0]
    sources = jnp.mod(sinks - tile_sep, time_count)

    def holder_block(items):
        tiles, sink_ids, source_ids, diagram = items
        return contract_tiles(gathered[sink_ids], gathered[source_ids], tiles, diagram)

    correlator = run_blocks(holder_block, (perambulator, sinks, sources, tile_diagram), tile_count)
    return (elemental, correlator)


CHUNKS = 2
VMEM_BLOCKS = 8 * 1024 * 1024


def factors(count):
    chips = count // 2
    inner = 1
    while inner * inner * 4 <= chips:
        inner *= 2
    while chips % inner:
        inner //= 2
    return (chips // inner, inner)


def fits(mesh, eigvecs):
    count = mesh.shape["space"]
    outer, inner = factors(count)
    total = eigvecs.size * eigvecs.dtype.itemsize // mesh.shape["groups"]
    return count % 2 == 0 and inner == 2 and outer >= 2 and total <= VMEM_BLOCKS


def kernel(
    dims,
    eig_ref,
    phase_ref,
    tiles_ref,
    sink_ref,
    sep_ref,
    diag_ref,
    elem_ref,
    corr_ref,
    held,
    left,
    right,
    cos_rows,
    sin_rows,
    mats,
    tile_mats,
    rows_re,
    rows_im,
    send_sem,
    recv_sem,
    tile_sem,
    own_sem,
):
    outer, inner, times, rows, nvec, tile_count = dims
    me = lax.axis_index("space")
    core = lax.rem(me, 2)
    chip = lax.div(me, 2)
    near = lax.rem(chip, inner)
    far = lax.div(chip, inner)
    sites = phase_ref.shape[1]
    per_site = rows // (sites // (outer * inner * 2))
    groups = rows // 8
    part = times // CHUNKS * groups
    pair = 2 * rows

    def index(far_pos, near_pos, core_pos):
        return (far_pos * inner + near_pos) * 2 + core_pos

    sibling = index(far, near, 1 - core)
    beside = index(far, 1 - near, core)
    above = index(far + 1, near, core)
    below = index(far - 1, near, core)
    has_above = far < outer - 1
    has_below = far > 0

    def tile_copies():
        full = slice(0, nvec)
        rest = slice(nvec, 2 * nvec)
        return [
            pltpu.make_async_copy(tiles_ref.at[:, 0], tile_mats.at[:, full, full], tile_sem.at[0]),
            pltpu.make_async_copy(tiles_ref.at[:, 1], tile_mats.at[:, full, rest], tile_sem.at[1]),
            pltpu.make_async_copy(tiles_ref.at[:, 0], tile_mats.at[:, rest, rest], tile_sem.at[2]),
        ]

    own_copy = pltpu.make_async_copy(eig_ref, held.at[me], own_sem)
    own_copy.start()
    for copy in tile_copies():
        copy.start()

    barrier = pltpu.get_barrier_semaphore()

    def greet(target):
        pl.semaphore_signal(barrier, inc=1, device_id={"space": target}, device_id_type=pl.DeviceIdType.MESH)

    greet(sibling)
    greet(beside)

    @pl.when(has_above)
    def _():
        greet(above)

    @pl.when(has_below)
    def _():
        greet(below)

    pl.semaphore_wait(barrier, 2 + has_above.astype(jnp.int32) + has_below.astype(jnp.int32))

    def piece(ref, chunk):
        return ref.at[pl.ds(chunk * part, part)]

    def remote(way, target, origin, chunk, own=False):
        return pltpu.make_async_remote_copy(
            src_ref=piece(eig_ref, chunk) if own else piece(held.at[origin], chunk),
            dst_ref=piece(held.at[origin], chunk),
            send_sem=send_sem.at[way, origin, chunk],
            recv_sem=recv_sem.at[origin, chunk],
            device_id={"space": target},
            device_id_type=pl.DeviceIdType.MESH,
        )

    def arrived(origin, chunk):
        remote(0, sibling, origin, chunk).wait_recv()

    for chunk in range(CHUNKS):
        @pl.when(has_above)
        def _():
            remote(2, above, me, chunk, own=True).start()

        @pl.when(has_below)
        def _():
            remote(3, below, me, chunk, own=True).start()

        remote(1, beside, me, chunk, own=True).start()
        remote(0, sibling, me, chunk, own=True).start()

    angle = 2.0 * math.pi / PERIOD * phase_ref[...].astype(jnp.float32)
    total_rows = sites * per_site
    row_id = lax.broadcasted_iota(jnp.int32, (total_rows, sites), 0)
    first_row = lax.broadcasted_iota(jnp.int32, (total_rows, sites), 1) * per_site
    chosen = (row_id >= first_row) & (row_id < first_row + per_site)

    def spread(values):
        column = jnp.sum(jnp.where(chosen, values, 0.0), axis=1, keepdims=True)
        return jnp.broadcast_to(column, (total_rows, nvec))

    cos_rows[...] = spread(jnp.cos(angle))
    sin_rows[...] = spread(jnp.sin(angle))
    own_copy.wait()

    def line_step(dist):
        def upward(start):
            for chunk in range(CHUNKS):
                origin = index(far - dist, near, core)
                if start:
                    arrived(origin, chunk)

                    @pl.when(has_above)
                    def _():
                        remote(2, above, origin, chunk).start()

                    remote(1, beside, origin, chunk).start()
                    remote(0, sibling, origin, chunk).start()

        def downward(start):
            for chunk in range(CHUNKS):
                origin = index(far + dist, near, core)
                arrived(origin, chunk)

                @pl.when(has_below)
                def _():
                    remote(3, below, origin, chunk).start()

                remote(1, beside, origin, chunk).start()
                remote(0, sibling, origin, chunk).start()

        pl.when(far >= dist)(lambda: upward(True))
        pl.when(far + dist < outer)(lambda: downward(True))

    def beside_step(dist):
        def take(far_pos):
            for chunk in range(CHUNKS):
                origin = index(far_pos, 1 - near, core)
                arrived(origin, chunk)
                remote(0, sibling, origin, chunk).start()

        if dist == 0:
            take(far)
        else:
            pl.when(far >= dist)(lambda: take(far - dist))
            pl.when(far + dist < outer)(lambda: take(far + dist))

    even = lax.rem(lax.broadcasted_iota(jnp.int32, (pair, nvec), 0), 2) == 0

    def process(far_pos, near_pos):
        place = far_pos * inner + near_pos
        other = index(far_pos, near_pos, 1 - core)
        for chunk in range(CHUNKS):
            arrived(other, chunk)
        base = pl.multiple_of(place * pair, pair)
        cosine = cos_rows[pl.ds(base, pair), :]
        sine = sin_rows[pl.ds(base, pair), :]

        def one(time, carry):
            halves = [
                held[place * 2 + half, pl.ds(time * groups, groups)].astype(jnp.float32).reshape(rows, nvec)
                for half in range(2)
            ]
            vecs = jnp.concatenate(halves, axis=0)
            swapped = jnp.where(even, pltpu.roll(vecs, pair - 1, 0), -pltpu.roll(vecs, 1, 0))
            left[time, pl.ds(base, pair), :] = vecs.astype(jnp.bfloat16)
            right[time, pl.ds(base, pair), 0:nvec] = (cosine * vecs - sine * swapped).astype(jnp.bfloat16)
            right[time, pl.ds(base, pair), nvec:] = (sine * vecs + cosine * swapped).astype(jnp.bfloat16)
            return carry

        lax.fori_loop(0, times, one, 0, unroll=4)

    def process_at(dist, near_pos):
        if dist == 0:
            process(far, near_pos)
        else:
            pl.when(far >= dist)(lambda: process(far - dist, near_pos))
            pl.when(far + dist < outer)(lambda: process(far + dist, near_pos))

    process_at(0, near)
    line_step(1)
    beside_step(0)
    process_at(1, near)
    process_at(0, 1 - near)
    for dist in range(2, outer + 1):
        if dist < outer:
            line_step(dist)
        if dist == 2:
            for copy in tile_copies():
                copy.wait()
            tile_mats[:, nvec:, 0:nvec] = -tile_mats[:, 0:nvec, nvec:]
        beside_step(dist - 1)
        if dist < outer:
            process_at(dist, near)
        process_at(dist - 1, 1 - near)

    for time in range(times):
        value = lax.dot_general(
            left[time], right[time], (((0,), (0,)), ((), ())), preferred_element_type=jnp.float32
        )
        real_part = value[:, 0:nvec].astype(jnp.bfloat16)
        imag_part = value[:, nvec:].astype(jnp.bfloat16)
        mats[time, 0:nvec, 0:nvec] = real_part
        mats[time, 0:nvec, nvec:] = imag_part
        mats[time, nvec:, 0:nvec] = -imag_part
        mats[time, nvec:, nvec:] = real_part

    elem_ref[0, 0] = mats[me, 0:nvec, 0:nvec]
    elem_ref[0, 1] = mats[me, 0:nvec, nvec:]

    for tile in range(tile_count):
        sink = sink_ref[0, tile]
        source = lax.rem(sink - sep_ref[tile] + times, times)
        flag = diag_ref[tile] == 1
        first = jnp.where(flag, source, sink)
        second = jnp.where(flag, sink, source)
        ahead = jnp.dot(mats[first, 0:nvec, :], tile_mats[tile], preferred_element_type=jnp.float32)
        behind = jnp.dot(tile_mats[tile, 0:nvec, :], mats[second], preferred_element_type=jnp.float32)
        a_re, a_im = ahead[:, 0:nvec], ahead[:, nvec:]
        b_re, b_im = behind[:, 0:nvec], behind[:, nvec:]
        sign = jnp.where(flag, -1.0, 1.0)
        rows_re[tile : tile + 1, :] = jnp.sum(a_re * b_re + a_im * b_im, axis=0, keepdims=True)
        rows_im[tile : tile + 1, :] = sign * jnp.sum(a_im * b_re - a_re * b_im, axis=0, keepdims=True)

    corr_ref[:, 0:1] = jnp.sum(rows_re[...], axis=1, keepdims=True)
    corr_ref[:, 1:2] = jnp.sum(rows_im[...], axis=1, keepdims=True)

    def sent(way, origin):
        for chunk in range(CHUNKS):
            remote(way, sibling, origin, chunk).wait_send()

    sent(1, me)
    sent(0, me)
    pl.when(has_above)(lambda: sent(2, me))
    pl.when(has_below)(lambda: sent(3, me))
    sent(0, index(far, 1 - near, core))
    for dist in range(1, outer):
        @pl.when(far >= dist)
        def _():
            origin = index(far - dist, near, core)
            sent(0, origin)
            sent(1, origin)
            pl.when(has_above)(lambda: sent(2, origin))
            sent(0, index(far - dist, 1 - near, core))

        @pl.when(far + dist < outer)
        def _():
            origin = index(far + dist, near, core)
            sent(0, origin)
            sent(1, origin)
            pl.when(has_below)(lambda: sent(3, origin))
            sent(0, index(far + dist, 1 - near, core))


def local_small(count, eigvecs, phase_index, perambulator, tile_sink, tile_sep, tile_diagram):
    times, sites, parts, colors, nvec = eigvecs.shape
    rows = sites * parts * colors
    tile_count = perambulator.shape[0]
    outer, inner = factors(count)
    flat = jnp.transpose(eigvecs, (0, 1, 3, 2, 4)).reshape(times * rows // 8, 8, nvec)
    vmem = pl.BlockSpec(memory_space=pltpu.VMEM)
    smem = pl.BlockSpec(memory_space=pltpu.SMEM)
    hbm = pl.BlockSpec(memory_space=pl.ANY)
    depth = count * rows
    return pl.pallas_call(
        functools.partial(kernel, (outer, inner, times, rows, nvec, tile_count)),
        out_shape=(
            jax.ShapeDtypeStruct((1, 2, nvec, nvec), jnp.bfloat16),
            jax.ShapeDtypeStruct((tile_count, 2), jnp.float32),
        ),
        in_specs=[vmem, vmem, hbm, smem, smem, smem],
        out_specs=(vmem, vmem),
        scratch_shapes=[
            pltpu.VMEM((count, times * rows // 8, 8, nvec), jnp.bfloat16),
            pltpu.VMEM((times, depth, nvec), jnp.bfloat16),
            pltpu.VMEM((times, depth, 2 * nvec), jnp.bfloat16),
            pltpu.VMEM((depth, nvec), jnp.float32),
            pltpu.VMEM((depth, nvec), jnp.float32),
            pltpu.VMEM((times, 2 * nvec, 2 * nvec), jnp.bfloat16),
            pltpu.VMEM((tile_count, 2 * nvec, 2 * nvec), jnp.bfloat16),
            pltpu.VMEM((tile_count, nvec), jnp.float32),
            pltpu.VMEM((tile_count, nvec), jnp.float32),
            pltpu.SemaphoreType.DMA((4, count, CHUNKS)),
            pltpu.SemaphoreType.DMA((count, CHUNKS)),
            pltpu.SemaphoreType.DMA((3,)),
            pltpu.SemaphoreType.DMA,
        ],
        compiler_params=pltpu.CompilerParams(collective_id=0, has_side_effects=True),
    )(flat, phase_index.reshape(1, -1), perambulator, tile_sink.reshape(1, -1), tile_sep, tile_diagram)


def solution(mesh):
    def program(*operands):
        if fits(mesh, operands[0]):
            body = functools.partial(local_small, mesh.shape["space"])
        else:
            body = local_large
        mapped = jax.shard_map(
            body,
            mesh=mesh,
            in_specs=(
                P("groups", "space", None, None, None),
                P("groups"),
                P(("groups", "space"), None, None, None),
                P(("groups", "space"), None),
                P(("groups", "space")),
                P(("groups", "space")),
            ),
            out_specs=(P(("groups", "space"), None, None, None), P(("groups", "space"), None)),
            check_vma=False,
        )
        return mapped(*operands)

    return program
```

```python
import functools
import math

import jax
import jax.numpy as jnp
from jax import lax
from jax.experimental import pallas as pl
from jax.experimental.pallas import tpu as pltpu
from jax.sharding import PartitionSpec as P

PERIOD = 48


def make_right(vecs, cosine, sine):
    real_part = vecs[..., 0, :, :].astype(jnp.float32)
    imag_part = vecs[..., 1, :, :].astype(jnp.float32)
    cos_col = cosine[:, None, None]
    sin_col = sine[:, None, None]
    first = (cos_col * real_part - sin_col * imag_part).astype(jnp.bfloat16)
    second = (sin_col * real_part + cos_col * imag_part).astype(jnp.bfloat16)
    top = jnp.stack([first, second], -2)
    bottom = jnp.stack([second, -first], -2)
    return jnp.stack([top, bottom], -4)


def phases(indices):
    angle = 2.0 * math.pi / PERIOD * indices.astype(jnp.float32)
    return (jnp.cos(angle), jnp.sin(angle))


def contract_tiles(sink_mat, source_mat, tiles, diagram):

    def mult(left, right):
        return jnp.einsum("bij,bjk->bik", left, right, preferred_element_type=jnp.float32)

    tile_re = tiles[:, 0]
    tile_im = tiles[:, 1]
    trans_re = jnp.swapaxes(tile_re, 1, 2)
    trans_im = -jnp.swapaxes(tile_im, 1, 2)
    flag = (diagram == 1)[:, None, None]
    left_re = jnp.where(flag, trans_re, tile_re)
    left_im = jnp.where(flag, trans_im, tile_im)
    right_re = jnp.where(flag, tile_re, trans_re)
    right_im = jnp.where(flag, tile_im, trans_im)
    sink_re = sink_mat[:, 0]
    sink_im = sink_mat[:, 1]
    src_re = jnp.swapaxes(source_mat[:, 0], 1, 2)
    src_im = -jnp.swapaxes(source_mat[:, 1], 1, 2)
    first_re = mult(sink_re, left_re) - mult(sink_im, left_im)
    first_im = mult(sink_re, left_im) + mult(sink_im, left_re)
    second_re = jnp.swapaxes(mult(src_re, right_re) - mult(src_im, right_im), 1, 2)
    second_im = jnp.swapaxes(mult(src_re, right_im) + mult(src_im, right_re), 1, 2)
    trace_re = jnp.sum(first_re * second_re - first_im * second_im, axis=(1, 2))
    trace_im = jnp.sum(first_re * second_im + first_im * second_re, axis=(1, 2))
    return jnp.stack([trace_re, trace_im], -1)


def run_blocks(step_fn, items, total):
    block = math.gcd(32, total)
    shaped = tuple((item.reshape((total // block, block) + item.shape[1:]) for item in items))
    result = lax.map(step_fn, shaped)
    return result.reshape((total,) + result.shape[2:])


def local_large(eigvecs, phase_index, perambulator, tile_sink, tile_sep, tile_diagram):
    tile_count = perambulator.shape[0]
    sinks = tile_sink[:, 0]
    cosine, sine = phases(phase_index)
    slices = lax.all_to_all(eigvecs, "space", split_axis=0, concat_axis=1, tiled=True)
    vecs = slices[0]
    right = make_right(vecs, cosine, sine)
    value = jnp.einsum("spck,spcol->okl", vecs, right, preferred_element_type=jnp.float32)
    elemental = value.astype(jnp.bfloat16)[None]
    gathered = lax.all_gather(elemental, "space", axis=0, tiled=True)
    time_count = gathered.shape[0]
    sources = jnp.mod(sinks - tile_sep, time_count)

    def holder_block(items):
        tiles, sink_ids, source_ids, diagram = items
        return contract_tiles(gathered[sink_ids], gathered[source_ids], tiles, diagram)

    correlator = run_blocks(holder_block, (perambulator, sinks, sources, tile_diagram), tile_count)
    return (elemental, correlator)


CHUNKS = 1
VMEM_BLOCKS = 8 * 1024 * 1024


def factors(count):
    chips = count // 2
    inner = 1
    while inner * inner * 4 <= chips:
        inner *= 2
    while chips % inner:
        inner //= 2
    return (chips // inner, inner)


def fits(mesh, eigvecs):
    count = mesh.shape["space"]
    outer, inner = factors(count)
    total = eigvecs.size * eigvecs.dtype.itemsize // mesh.shape["groups"]
    return count % 2 == 0 and inner == 2 and outer >= 2 and total <= VMEM_BLOCKS


def kernel(
    dims,
    eig_ref,
    phase_hbm,
    mats,
    held,
    left,
    right,
    cos_rows,
    sin_rows,
    send_sem,
    recv_sem,
    own_sem,
    phase_ref,
    phase_sem,
):
    outer, inner, times, rows, nvec = dims
    me = lax.axis_index("space")
    core = lax.rem(me, 2)
    chip = lax.div(me, 2)
    near = lax.rem(chip, inner)
    far = lax.div(chip, inner)
    sites = phase_ref.shape[1]
    per_site = rows // (sites // (outer * inner * 2))
    groups = rows // 8
    part = times // CHUNKS * groups
    pair = 2 * rows

    def index(far_pos, near_pos, core_pos):
        return (far_pos * inner + near_pos) * 2 + core_pos

    sibling = index(far, near, 1 - core)
    beside = index(far, 1 - near, core)
    above = index(far + 1, near, core)
    below = index(far - 1, near, core)
    has_above = far < outer - 1
    has_below = far > 0

    own_copy = pltpu.make_async_copy(eig_ref, held.at[me], own_sem)
    own_copy.start()
    phase_copy = pltpu.make_async_copy(phase_hbm, phase_ref, phase_sem)
    phase_copy.start()

    barrier = pltpu.get_barrier_semaphore()

    def greet(target):
        pl.semaphore_signal(barrier, inc=1, device_id={"space": target}, device_id_type=pl.DeviceIdType.MESH)

    greet(sibling)
    greet(beside)

    @pl.when(has_above)
    def _():
        greet(above)

    @pl.when(has_below)
    def _():
        greet(below)

    pl.semaphore_wait(barrier, 2 + has_above.astype(jnp.int32) + has_below.astype(jnp.int32))

    def piece(ref, chunk):
        return ref.at[pl.ds(chunk * part, part)]

    def remote(way, target, origin, chunk, own=False):
        return pltpu.make_async_remote_copy(
            src_ref=piece(eig_ref, chunk) if own else piece(held.at[origin], chunk),
            dst_ref=piece(held.at[origin], chunk),
            send_sem=send_sem.at[way, origin, chunk],
            recv_sem=recv_sem.at[origin, chunk],
            device_id={"space": target},
            device_id_type=pl.DeviceIdType.MESH,
        )

    def arrived(origin, chunk):
        remote(0, sibling, origin, chunk).wait_recv()

    for chunk in range(CHUNKS):
        @pl.when(has_above)
        def _():
            remote(2, above, me, chunk, own=True).start()

        @pl.when(has_below)
        def _():
            remote(3, below, me, chunk, own=True).start()

        remote(1, beside, me, chunk, own=True).start()
        remote(0, sibling, me, chunk, own=True).start()

    phase_copy.wait()
    angle = 2.0 * math.pi / PERIOD * phase_ref[...].astype(jnp.float32)
    total_rows = sites * per_site
    row_id = lax.broadcasted_iota(jnp.int32, (total_rows, sites), 0)
    first_row = lax.broadcasted_iota(jnp.int32, (total_rows, sites), 1) * per_site
    chosen = (row_id >= first_row) & (row_id < first_row + per_site)

    def spread(values):
        column = jnp.sum(jnp.where(chosen, values, 0.0), axis=1, keepdims=True)
        return jnp.broadcast_to(column, (total_rows, nvec))

    cos_rows[...] = spread(jnp.cos(angle))
    sin_rows[...] = spread(jnp.sin(angle))
    own_copy.wait()

    def line_step(dist):
        def upward(start):
            for chunk in range(CHUNKS):
                origin = index(far - dist, near, core)
                if start:
                    arrived(origin, chunk)

                    @pl.when(has_above)
                    def _():
                        remote(2, above, origin, chunk).start()

                    remote(1, beside, origin, chunk).start()
                    remote(0, sibling, origin, chunk).start()

        def downward(start):
            for chunk in range(CHUNKS):
                origin = index(far + dist, near, core)
                arrived(origin, chunk)

                @pl.when(has_below)
                def _():
                    remote(3, below, origin, chunk).start()

                remote(1, beside, origin, chunk).start()
                remote(0, sibling, origin, chunk).start()

        pl.when(far >= dist)(lambda: upward(True))
        pl.when(far + dist < outer)(lambda: downward(True))

    def beside_step(dist):
        def take(far_pos):
            for chunk in range(CHUNKS):
                origin = index(far_pos, 1 - near, core)
                arrived(origin, chunk)
                remote(0, sibling, origin, chunk).start()

        if dist == 0:
            take(far)
        else:
            pl.when(far >= dist)(lambda: take(far - dist))
            pl.when(far + dist < outer)(lambda: take(far + dist))

    even = lax.rem(lax.broadcasted_iota(jnp.int32, (pair, nvec), 0), 2) == 0

    def process(far_pos, near_pos):
        place = far_pos * inner + near_pos
        other = index(far_pos, near_pos, 1 - core)
        for chunk in range(CHUNKS):
            arrived(other, chunk)
        base = pl.multiple_of(place * pair, pair)
        cosine = cos_rows[pl.ds(base, pair), :]
        sine = sin_rows[pl.ds(base, pair), :]

        def one(time, carry):
            halves = [
                held[place * 2 + half, pl.ds(time * groups, groups)].astype(jnp.float32).reshape(rows, nvec)
                for half in range(2)
            ]
            vecs = jnp.concatenate(halves, axis=0)
            swapped = jnp.where(even, pltpu.roll(vecs, pair - 1, 0), -pltpu.roll(vecs, 1, 0))
            left[time, pl.ds(base, pair), :] = vecs.astype(jnp.bfloat16)
            right[time, pl.ds(base, pair), 0:nvec] = (cosine * vecs - sine * swapped).astype(jnp.bfloat16)
            right[time, pl.ds(base, pair), nvec:] = (sine * vecs + cosine * swapped).astype(jnp.bfloat16)
            return carry

        lax.fori_loop(0, times, one, 0, unroll=4)

    def process_at(dist, near_pos):
        if dist == 0:
            process(far, near_pos)
        else:
            pl.when(far >= dist)(lambda: process(far - dist, near_pos))
            pl.when(far + dist < outer)(lambda: process(far + dist, near_pos))

    process_at(0, near)
    line_step(1)
    beside_step(0)
    process_at(1, near)
    process_at(0, 1 - near)
    for dist in range(2, outer + 1):
        if dist < outer:
            line_step(dist)
        beside_step(dist - 1)
        if dist < outer:
            process_at(dist, near)
        process_at(dist - 1, 1 - near)

    for time in range(times):
        value = lax.dot_general(
            left[time], right[time], (((0,), (0,)), ((), ())), preferred_element_type=jnp.float32
        )
        real_part = value[:, 0:nvec].astype(jnp.bfloat16)
        imag_part = value[:, nvec:].astype(jnp.bfloat16)
        mats[time, 0:nvec, 0:nvec] = real_part
        mats[time, 0:nvec, nvec:] = imag_part
        mats[time, nvec:, 0:nvec] = -imag_part
        mats[time, nvec:, nvec:] = real_part

    def sent(way, origin):
        for chunk in range(CHUNKS):
            remote(way, sibling, origin, chunk).wait_send()

    sent(1, me)
    sent(0, me)
    pl.when(has_above)(lambda: sent(2, me))
    pl.when(has_below)(lambda: sent(3, me))
    sent(0, index(far, 1 - near, core))
    for dist in range(1, outer):
        @pl.when(far >= dist)
        def _():
            origin = index(far - dist, near, core)
            sent(0, origin)
            sent(1, origin)
            pl.when(has_above)(lambda: sent(2, origin))
            sent(0, index(far - dist, 1 - near, core))

        @pl.when(far + dist < outer)
        def _():
            origin = index(far + dist, near, core)
            sent(0, origin)
            sent(1, origin)
            pl.when(has_below)(lambda: sent(3, origin))
            sent(0, index(far + dist, 1 - near, core))


def contract_kernel(mats, tiles_ref, sink_ref, sep_ref, diag_ref, elem_ref, corr_ref, rows_re, rows_im):
    me = lax.axis_index("space")
    times = mats.shape[0]
    tile_count, _, nvec, _ = tiles_ref.shape
    elem_ref[0, 0] = mats[me, 0:nvec, 0:nvec]
    elem_ref[0, 1] = mats[me, 0:nvec, nvec:]

    for tile in range(tile_count):
        sink = sink_ref[0, tile]
        source = lax.rem(sink - sep_ref[tile] + times, times)
        flag = diag_ref[tile] == 1
        first = jnp.where(flag, source, sink)
        second = jnp.where(flag, sink, source)
        top = jnp.concatenate([tiles_ref[tile, 0], tiles_ref[tile, 1]], axis=1)
        both = jnp.concatenate([top, jnp.concatenate([-tiles_ref[tile, 1], tiles_ref[tile, 0]], axis=1)], axis=0)
        ahead = jnp.dot(mats[first, 0:nvec, :], both, preferred_element_type=jnp.float32)
        behind = jnp.dot(top, mats[second], preferred_element_type=jnp.float32)
        a_re, a_im = ahead[:, 0:nvec], ahead[:, nvec:]
        b_re, b_im = behind[:, 0:nvec], behind[:, nvec:]
        sign = jnp.where(flag, -1.0, 1.0)
        rows_re[tile : tile + 1, :] = jnp.sum(a_re * b_re + a_im * b_im, axis=0, keepdims=True)
        rows_im[tile : tile + 1, :] = sign * jnp.sum(a_im * b_re - a_re * b_im, axis=0, keepdims=True)

    corr_ref[0] = jnp.sum(rows_re[...], axis=1)
    corr_ref[1] = jnp.sum(rows_im[...], axis=1)


def local_small(count, eigvecs, phase_index, perambulator, tile_sink, tile_sep, tile_diagram):
    times, sites, parts, colors, nvec = eigvecs.shape
    rows = sites * parts * colors
    tile_count = perambulator.shape[0]
    outer, inner = factors(count)
    flat = jnp.transpose(eigvecs, (0, 1, 3, 2, 4)).reshape(times * rows // 8, 8, nvec)
    vmem = pl.BlockSpec(memory_space=pltpu.VMEM)
    hbm = pl.BlockSpec(memory_space=pltpu.HBM)
    smem = pl.BlockSpec(memory_space=pltpu.SMEM)
    depth = count * rows
    mats = pl.pallas_call(
        functools.partial(kernel, (outer, inner, times, rows, nvec)),
        out_shape=jax.ShapeDtypeStruct((times, 2 * nvec, 2 * nvec), jnp.bfloat16),
        in_specs=[hbm, hbm],
        out_specs=vmem,
        scratch_shapes=[
            pltpu.VMEM((count, times * rows // 8, 8, nvec), jnp.bfloat16),
            pltpu.VMEM((times, depth, nvec), jnp.bfloat16),
            pltpu.VMEM((times, depth, 2 * nvec), jnp.bfloat16),
            pltpu.VMEM((depth, nvec), jnp.float32),
            pltpu.VMEM((depth, nvec), jnp.float32),
            pltpu.SemaphoreType.DMA((4 + 2 * outer, count, CHUNKS)),
            pltpu.SemaphoreType.DMA((count, CHUNKS)),
            pltpu.SemaphoreType.DMA,
            pltpu.VMEM((1, phase_index.shape[0]), jnp.int32),
            pltpu.SemaphoreType.DMA,
        ],
        compiler_params=pltpu.CompilerParams(
            collective_id=0, has_side_effects=True, vmem_limit_bytes=24 * 1024 * 1024
        ),
    )(pltpu.with_memory_space_constraint(flat, pltpu.HBM), pltpu.with_memory_space_constraint(phase_index.reshape(1, -1), pltpu.HBM))
    elementals, correlator = pl.pallas_call(
        contract_kernel,
        out_shape=(
            jax.ShapeDtypeStruct((1, 2, nvec, nvec), jnp.bfloat16),
            jax.ShapeDtypeStruct((2, tile_count), jnp.float32),
        ),
        in_specs=[vmem, vmem, smem, smem, smem],
        out_specs=(vmem, vmem),
        scratch_shapes=[
            pltpu.VMEM((tile_count, nvec), jnp.float32),
            pltpu.VMEM((tile_count, nvec), jnp.float32),
        ],
        compiler_params=pltpu.CompilerParams(vmem_limit_bytes=24 * 1024 * 1024),
    )(mats, perambulator, tile_sink.reshape(1, -1), tile_sep, tile_diagram)
    return (elementals, correlator.T)


def solution(mesh):
    def program(*operands):
        if fits(mesh, operands[0]):
            body = functools.partial(local_small, mesh.shape["space"])
        else:
            body = local_large
        mapped = jax.shard_map(
            body,
            mesh=mesh,
            in_specs=(
                P("groups", "space", None, None, None),
                P("groups"),
                P(("groups", "space"), None, None, None),
                P(("groups", "space"), None),
                P(("groups", "space")),
                P(("groups", "space")),
            ),
            out_specs=(P(("groups", "space"), None, None, None), P(("groups", "space"), None)),
            check_vma=False,
        )
        return mapped(*operands)

    return program
```
